1024 devices in a mesh: ctx: 128 (over x, y, z_lo), tp: 8 (over z_hi, core).
Axes of the slice: x: 4, y: 4, z: 32 (z_hi: 4, z_lo: 8; z = z_hi * 8 + z_lo), core: 2. Of those that a mesh axis runs over, the one named last changes fastest.
Arguments:
- queries: bfloat16 [2, 128, 128, 8192], P(None, 'ctx', None, 'tp'), may hold values from -5 to 5
- keys: bfloat16 [2, 128, 128, 1024], P(None, 'ctx', None, 'tp'), may hold values from -5 to 5
- values: bfloat16 [2, 128, 128, 1024], P(None, 'ctx', None, 'tp'), may hold values from -6 to 6
- out_grad: bfloat16 [2, 128, 128, 8192], P(None, 'ctx', None, 'tp'), may hold values from -6 to 6
- block_doc: int32 [256], replicated, may hold values from 0 to 255, as said below
Outputs:
- attn_out: bfloat16 [2, 128, 128, 8192], P(None, 'ctx', None, 'tp')
- query_grad: bfloat16 [2, 128, 128, 8192], P(None, 'ctx', None, 'tp')
- key_grad: bfloat16 [2, 128, 128, 1024], P(None, 'ctx', None, 'tp')
- value_grad: bfloat16 [2, 128, 128, 1024], P(None, 'ctx', None, 'tp')
The draws below stay inside these ranges and needn't reach their ends.
Inputs may be any that keep to these rules, and one draw needn't show every extreme that they name: block_doc never falls along the sequence; each document covers 1 to 8 consecutive blocks, and in each half of the sequence the first document covers exactly 8; no document holds both block 127 and block 128; the first block's id is 0 and the last block's id is 255.
All inputs are finite; a program needn't handle non-finite values.
Results may differ from the reference program's by a relative error of at most 0.0094.
Values may be sent and summed in bfloat16 or wider, within the bound.
A program may use at most 32 MiB of HBM per device.

```python
import math
import jax
import jax.numpy as jnp
from jax import lax

HQ = 64
HK = 8
HD = 128
BLOCK = 128
PIECE = 128
GROUP = 8
SEQ = 32768
NBLK = 256
MAXB = 8
N_CTX = 128


def draw_queries(key, part):
    pair_count = SEQ // (2 * PIECE)
    full_shape = (2, pair_count, PIECE, HQ * HD)
    return jnp.clip(jax.random.normal(jax.random.fold_in(key, 11), full_shape, jnp.float32), -5.0, 5.0).astype(jnp.bfloat16)


def draw_keys(key, part):
    pair_count = SEQ // (2 * PIECE)
    full_shape = (2, pair_count, PIECE, HK * HD)
    return jnp.clip(jax.random.normal(jax.random.fold_in(key, 31), full_shape, jnp.float32), -5.0, 5.0).astype(jnp.bfloat16)


def draw_block_doc(key, part):
    half_blocks = NBLK // 2

    def one_half(sub_key):
        lengths = jax.random.randint(sub_key, (half_blocks,), 1, MAXB + 1)
        lengths = jnp.where(jnp.arange(half_blocks) == 0, MAXB, lengths)
        starts = jnp.cumsum(lengths) - lengths
        blocks = jnp.arange(half_blocks)
        return jnp.sum((starts[None, :] <= blocks[:, None]).astype(jnp.int32), axis=1) - 1
    first_half = one_half(jax.random.fold_in(key, 21))
    second_local = one_half(jax.random.fold_in(key, 22))
    second_count = second_local[half_blocks - 1] + 1
    second_half = second_local + (NBLK - second_count)
    return jnp.concatenate([first_half, second_half]).astype(jnp.int32)


def block_levels(own_key, dims, pieces, least, largest):
    level = 1.0
    for position, shards_of in pieces:
        draws = jax.random.uniform(jax.random.fold_in(jax.random.fold_in(own_key, 6), position), (shards_of,), jnp.float32, least / len(pieces), largest / len(pieces))
        level = level * jnp.repeat(jnp.exp(draws), dims[position] // shards_of).reshape((-1,) + (1,) * (len(dims) - 1 - position))
    return level


def noise(key, dims, scale, most, split=(), kind=jnp.bfloat16):
    loudness = block_levels(key, dims, split, -0.22, 0.18) if split else 1.0
    array = jax.random.normal(key, dims, jnp.float32) * scale * loudness
    return jnp.minimum(jnp.maximum(array, -most), most).astype(kind)


def setup_inputs(seed: int = 0) -> dict:
    seeds = jax.random.split(jax.random.key(seed), 6)
    queries = draw_queries(jax.random.fold_in(seeds[5], 71), 0)
    keys = draw_keys(jax.random.fold_in(seeds[5], 71), 0)
    values = noise(seeds[2], (2, N_CTX, PIECE, HK * HD), 1.0, 6.0, ((1, 128), (3, 8)))
    out_grad = noise(seeds[3], (2, N_CTX, PIECE, HQ * HD), 1.0, 6.0, ((1, 128), (3, 8)))
    block_doc = draw_block_doc(jax.random.fold_in(seeds[5], 71), 0)
    return dict(queries=queries, keys=keys, values=values, out_grad=out_grad, block_doc=block_doc)


masked_score = -1e+30

def to_sequence(arranged):
    return jnp.concatenate([arranged[0], arranged[1][::-1]], axis=0)

def to_pairs(ordered, pair_count):
    return jnp.stack([ordered[:pair_count], ordered[pair_count:][::-1]])

def reference(queries, keys, values, out_grad, block_doc):
    pair_count = queries.shape[1]
    scaling = 1.0 / math.sqrt(HD)
    padding = MAXB - 1
    query_seq = to_sequence(queries).reshape(NBLK, BLOCK, HK, GROUP, HD)
    grad_seq = to_sequence(out_grad).reshape(NBLK, BLOCK, HK, GROUP, HD)
    key_seq = to_sequence(keys).reshape(NBLK, BLOCK, HK, HD)
    value_seq = to_sequence(values).reshape(NBLK, BLOCK, HK, HD)
    key_pad = jnp.concatenate([jnp.zeros((padding, BLOCK, HK, HD), key_seq.dtype), key_seq], axis=0)
    value_pad = jnp.concatenate([jnp.zeros((padding, BLOCK, HK, HD), value_seq.dtype), value_seq], axis=0)
    doc_pad = jnp.concatenate([jnp.full((padding,), -1, jnp.int32), block_doc.astype(jnp.int32)])
    offsets = jnp.arange(BLOCK, dtype=jnp.int32)
    window_offsets = jnp.arange(MAXB * BLOCK, dtype=jnp.int32)

    def visit(carry, block_index):
        key_acc, value_acc = carry
        query_block = lax.dynamic_index_in_dim(query_seq, block_index, 0, keepdims=False).astype(jnp.float32)
        grad_block = lax.dynamic_index_in_dim(grad_seq, block_index, 0, keepdims=False).astype(jnp.float32)
        key_window = lax.dynamic_slice_in_dim(key_pad, block_index, MAXB, 0).reshape(MAXB * BLOCK, HK, HD).astype(jnp.float32)
        value_window = lax.dynamic_slice_in_dim(value_pad, block_index, MAXB, 0).reshape(MAXB * BLOCK, HK, HD).astype(jnp.float32)
        key_docs = jnp.repeat(lax.dynamic_slice_in_dim(doc_pad, block_index, MAXB, 0), BLOCK)
        query_doc = lax.dynamic_index_in_dim(block_doc.astype(jnp.int32), block_index, 0, keepdims=False)
        query_pos = block_index * BLOCK + offsets
        key_pos = (block_index - padding) * BLOCK + window_offsets
        visible = (key_docs[None, :] == query_doc) & (key_pos[None, :] <= query_pos[:, None])
        scores = jnp.einsum('qhgd,khd->hgqk', query_block, key_window) * scaling
        scores = jnp.where(visible, scores, masked_score)
        row_max = lax.optimization_barrier(jnp.max(scores, axis=-1, keepdims=True))
        log_total = row_max + jnp.log(lax.optimization_barrier(jnp.sum(jnp.exp(scores - row_max), axis=-1, keepdims=True)))
        probs = jnp.exp(scores - log_total)
        probs_low = lax.optimization_barrier(probs.astype(jnp.bfloat16)).astype(jnp.float32)
        attended = jnp.einsum('hgqk,khd->qhgd', probs_low, value_window)
        out_low = attended.astype(jnp.bfloat16)
        out_back = lax.optimization_barrier(out_low).astype(jnp.float32)
        delta = jnp.einsum('qhgd,qhgd->hgq', grad_block, out_back)
        dprobs = jnp.einsum('qhgd,khd->hgqk', grad_block, value_window)
        dscores = lax.optimization_barrier((probs * (dprobs - delta[..., None])).astype(jnp.bfloat16)).astype(jnp.float32)
        query_part = jnp.einsum('hgqk,khd->qhgd', dscores, key_window) * scaling
        key_part = (jnp.einsum('hgqk,qhgd->khd', dscores, query_block) * scaling).reshape(MAXB, BLOCK, HK, HD)
        value_part = jnp.einsum('hgqk,qhgd->khd', probs_low, grad_block).reshape(MAXB, BLOCK, HK, HD)
        key_acc = lax.dynamic_update_slice_in_dim(key_acc, lax.dynamic_slice_in_dim(key_acc, block_index, MAXB, 0) + key_part, block_index, 0)
        value_acc = lax.dynamic_update_slice_in_dim(value_acc, lax.dynamic_slice_in_dim(value_acc, block_index, MAXB, 0) + value_part, block_index, 0)
        return ((key_acc, value_acc), (out_low, query_part.astype(jnp.bfloat16)))
    zero_acc = jnp.zeros((NBLK + padding, BLOCK, HK, HD), jnp.float32)
    (key_acc, value_acc), (outs_all, qgrads_all) = lax.scan(visit, (zero_acc, zero_acc), jnp.arange(NBLK, dtype=jnp.int32))
    attn_out = to_pairs(outs_all.reshape(2 * pair_count, PIECE, HQ * HD), pair_count)
    query_grad = to_pairs(qgrads_all.reshape(2 * pair_count, PIECE, HQ * HD), pair_count)
    key_grad = to_pairs(key_acc[padding:].astype(jnp.bfloat16).reshape(2 * pair_count, PIECE, HK * HD), pair_count)
    value_grad = to_pairs(value_acc[padding:].astype(jnp.bfloat16).reshape(2 * pair_count, PIECE, HK * HD), pair_count)
    return (attn_out, query_grad, key_grad, value_grad)
```

```python
import functools
import math

import jax
import jax.numpy as jnp
from jax import lax
from jax.experimental import pallas as pl
from jax.experimental.pallas import tpu as pltpu
from jax.sharding import PartitionSpec as P

HD = 128
GROUP = 8
TOK = 128
RUN = 8
COLS = GROUP * TOK
WIDE = 256
MASKED = -1e30
SCALE = 1.0 / math.sqrt(HD)
EXP2_SCALE = SCALE * math.log2(math.e)
UP, DOWN = 0, 1


def dot(left, right, left_dim, right_dim):
    return lax.dot_general(
        left, right, (((left_dim,), (right_dim,)), ((), ())), preferred_element_type=jnp.float32
    )


def rows_of(slot):
    return pl.ds(pl.multiple_of(slot * TOK, TOK), TOK)


def kernel(
    runs,
    doc_ref,
    q_hbm,
    k_hbm,
    v_hbm,
    g_hbm,
    out_ref,
    qgrad_ref,
    kgrad_ref,
    vgrad_ref,
    kv,
    kv_t,
    queries,
    grads,
    scores,
    dprobs,
    peak,
    probs,
    dscores,
    acc,
    own,
    snd,
    rcv,
    rcv_y,
    local_sem,
    load_sem,
    fetch_send,
    fetch_recv,
    fetch_y_send,
    fetch_y_recv,
    back_send,
    back_recv,
    back_y_send,
    back_y_recv,
):
    index = lax.axis_index("ctx")
    run = lax.div(index, RUN)
    place = lax.rem(index, RUN)
    next_run = lax.rem(run + 1, runs) * RUN + place
    last_run = lax.rem(run + runs - 1, runs) * RUN + place
    has_below = place >= 1
    has_above = place <= RUN - 2

    def copy(src, dst, send, recv, target):
        return pltpu.make_async_remote_copy(
            src_ref=src,
            dst_ref=dst,
            send_sem=send,
            recv_sem=recv,
            device_id={"ctx": target},
            device_id_type=pl.DeviceIdType.MESH,
        )

    kv_loads = []
    for piece in range(2):
        for part, source in enumerate((k_hbm, v_hbm)):
            kv_loads.append(
                pltpu.make_async_copy(
                    source.at[piece], kv.at[piece, place, part], local_sem.at[piece, part]
                )
            )
    for load in kv_loads:
        load.start()
    loads = []
    for piece in range(2):
        for which, (source, target) in enumerate(((q_hbm, queries), (g_hbm, grads))):
            for head in range(GROUP):
                span = pl.ds(head * TOK, TOK)
                loads.append(
                    pltpu.make_async_copy(
                        source.at[piece, :, span],
                        target.at[piece, span],
                        load_sem.at[piece, which, head],
                    )
                )
    for load in loads:
        load.start()

    barrier = pltpu.get_barrier_semaphore()

    def greet(target):
        pl.semaphore_signal(
            barrier, inc=1, device_id={"ctx": target}, device_id_type=pl.DeviceIdType.MESH
        )

    greet(next_run)
    greet(last_run)

    @pl.when(has_below)
    def _():
        greet(index - 1)

    @pl.when(has_above)
    def _():
        greet(index + 1)

    peers = 2 + has_below.astype(jnp.int32) + has_above.astype(jnp.int32)
    pl.semaphore_wait(barrier, peers)

    for load in kv_loads:
        load.wait()

    def fetch_y(piece):
        return copy(
            kv.at[piece, place],
            kv.at[piece, RUN],
            fetch_y_send.at[piece],
            fetch_y_recv.at[piece],
            (next_run, last_run)[piece],
        )

    def fetch(direction, piece, step, source, slot):
        return copy(
            kv.at[piece, source],
            kv.at[piece, slot],
            fetch_send.at[direction, piece, step],
            fetch_recv.at[direction, piece, step],
            index + 1 if direction == UP else index - 1,
        )

    y_needed = (has_below, has_above)
    for piece in range(2):

        @pl.when(y_needed[piece])
        def _(piece=piece):
            fetch_y(piece).start()

    @pl.when(has_above)
    def _():
        fetch(UP, 0, 0, place, place).start()

    @pl.when(has_below)
    def _():
        fetch(DOWN, 1, 0, place, place).start()

    for load in loads:
        load.wait()

    def doc_of(piece, run_of_slot, slot):
        at = run_of_slot * RUN + slot
        inside = (at >= 0) & (at < runs * RUN)
        at = jnp.clip(at, 0, runs * RUN - 1)
        block = at if piece == 0 else 2 * runs * RUN - 1 - at
        return jnp.where(inside, doc_ref[block], -1)

    my_docs = [doc_of(piece, run, place) for piece in range(2)]
    key_row = lax.broadcasted_iota(jnp.int32, (TOK, WIDE), 0)
    query_row = lax.rem(lax.broadcasted_iota(jnp.int32, (TOK, WIDE), 1), TOK)
    causal = key_row <= query_row

    def visit(slot, is_own):
        for piece in range(2):
            keys = kv[piece, slot, 0]
            vals = kv[piece, slot, 1]
            kv_t[piece, 0, :, rows_of(slot)] = keys.T
            kv_t[piece, 1, :, rows_of(slot)] = vals.T
            if not is_own:
                if piece == 0:
                    run_of_slot = jnp.where(slot > place, run - 1, run)
                else:
                    run_of_slot = jnp.where(slot < place, run + 1, run)
                doc = doc_of(piece, run_of_slot, slot)
                bias = jnp.where(doc == my_docs[piece], 0.0, MASKED)
            for first in range(0, COLS, WIDE):
                cols = pl.ds(first, WIDE)
                block = dot(keys, queries[piece, cols], 1, 1)
                if is_own:
                    block = jnp.where(causal, block, MASKED)
                else:
                    block = block + bias
                scores[piece, rows_of(slot), cols] = block
                top = jnp.max(block.reshape(TOK // 8, 8, WIDE), axis=0)
                if not is_own:
                    top = jnp.maximum(top, peak[piece, :, cols])
                peak[piece, :, cols] = top
                dprobs[piece, rows_of(slot), cols] = dot(vals, grads[piece, cols], 1, 1)

    visit(place, True)

    @pl.when(has_above)
    def _():
        fetch_y(1).wait_recv()
        fetch(UP, 1, 0, RUN, place).start()

    @pl.when(has_below)
    def _():
        fetch_y(0).wait_recv()
        fetch(DOWN, 0, 0, RUN, place).start()

    def fetch_step(step, carry):
        below = place - 1 - step
        above = place + 1 + step

        @pl.when(below >= 0)
        def _():
            for piece in range(2):
                fetch(UP, piece, step, below, below).wait_recv()

                @pl.when(has_above)
                def _(piece=piece):
                    fetch(UP, piece, step + 1, below, below).start()

        @pl.when(above < RUN)
        def _():
            for piece in (1, 0):
                fetch(DOWN, piece, step, above, above).wait_recv()

                @pl.when(has_below)
                def _(piece=piece):
                    fetch(DOWN, piece, step + 1, above, above).start()

        @pl.when(below >= 0)
        def _():
            visit(below, False)

        @pl.when(above < RUN)
        def _():
            visit(above, False)

        return carry

    lax.fori_loop(0, RUN - 1, fetch_step, 0)

    def soften(group, carry):
        for piece in range(2):
            cols = pl.ds(pl.multiple_of(group * WIDE, WIDE), WIDE)
            top = jnp.max(peak[piece, :, cols], axis=0, keepdims=True)
            total = jnp.zeros((8, WIDE), jnp.float32)
            delta = jnp.zeros((8, WIDE), jnp.float32)
            for slot in range(RUN):
                rows = pl.ds(slot * TOK, TOK)
                weight = jnp.exp2((scores[piece, rows, cols] - top) * EXP2_SCALE)
                scores[piece, rows, cols] = weight
                total += jnp.sum(weight.reshape(TOK // 8, 8, WIDE), axis=0)
                delta += jnp.sum(
                    (weight * dprobs[piece, rows, cols]).reshape(TOK // 8, 8, WIDE), axis=0
                )
            inverse = 1.0 / jnp.sum(total, axis=0, keepdims=True)
            delta = jnp.sum(delta, axis=0, keepdims=True) * inverse
            for slot in range(RUN):
                rows = pl.ds(slot * TOK, TOK)
                prob = scores[piece, rows, cols] * inverse
                probs[piece, rows, cols] = prob.astype(jnp.bfloat16)
                dscores[piece, rows, cols] = (prob * (dprobs[piece, rows, cols] - delta)).astype(
                    jnp.bfloat16
                )
        return carry

    lax.fori_loop(0, COLS // WIDE, soften, 0)

    def key_side(piece, slot):
        rows = rows_of(slot)
        return (
            dot(dscores[piece, rows, :], queries[piece], 1, 0) * SCALE,
            dot(probs[piece, rows, :], grads[piece], 1, 0),
        )

    def back(direction, piece, step, slot):
        return copy(
            snd.at[piece, slot],
            rcv.at[direction, piece, slot],
            back_send.at[direction, piece, step],
            back_recv.at[direction, piece, step],
            index + 1 if direction == UP else index - 1,
        )

    def back_step(step, carry):
        low = step - (RUN - 1) + place
        high = RUN - 1 - step + place
        todo = (
            (DOWN, low >= 0, low, has_above),
            (UP, high < RUN, high, has_below),
        )
        for direction, active, slot, _ in todo:

            @pl.when(active)
            def _(direction=direction, slot=slot):
                for piece in range(2):
                    for part, value in enumerate(key_side(piece, slot)):
                        acc[direction, piece, part] = value

        for direction, active, slot, receives in todo:

            @pl.when(active)
            def _(direction=direction, slot=slot, receives=receives):
                for piece in range(2):

                    @pl.when(receives)
                    def _(piece=piece):
                        back(direction, piece, step - 1, slot).wait_recv()
                        acc[direction, piece] += rcv[direction, piece, slot].astype(jnp.float32)

                    snd[piece, slot] = acc[direction, piece].astype(jnp.bfloat16)
                    back(direction, piece, step, slot).start()

        return carry

    lax.fori_loop(0, RUN - 1, back_step, 0)

    def back_y(piece):
        return copy(
            rcv.at[(UP, DOWN)[piece], piece, place],
            rcv_y.at[piece],
            back_y_send.at[piece],
            back_y_recv.at[piece],
            (last_run, next_run)[piece],
        )

    for piece in range(2):
        for part, value in enumerate(key_side(piece, place)):
            own[piece, part] = value

    @pl.when(has_below)
    def _():
        for piece in range(2):
            back(UP, piece, RUN - 2, place).wait_recv()
        back_y(0).start()
        own[1] += rcv[UP, 1, place].astype(jnp.float32)

    @pl.when(has_above)
    def _():
        for piece in (1, 0):
            back(DOWN, piece, RUN - 2, place).wait_recv()
        back_y(1).start()
        own[0] += rcv[DOWN, 0, place].astype(jnp.float32)

    def query_side(group, carry):
        for piece in range(2):
            cols = pl.ds(pl.multiple_of(group * WIDE, WIDE), WIDE)
            attended = dot(kv_t[piece, 1], probs[piece, :, cols], 1, 0)
            out_ref[piece, :, cols] = jnp.concatenate(
                [attended[:, :TOK].T, attended[:, TOK:].T], axis=1
            ).astype(jnp.bfloat16)
            pulled = dot(kv_t[piece, 0], dscores[piece, :, cols], 1, 0) * SCALE
            qgrad_ref[piece, :, cols] = jnp.concatenate(
                [pulled[:, :TOK].T, pulled[:, TOK:].T], axis=1
            ).astype(jnp.bfloat16)
        return carry

    lax.fori_loop(0, COLS // WIDE, query_side, 0)

    for piece in range(2):

        @pl.when(y_needed[piece])
        def _(piece=piece):
            back_y(piece).wait_recv()
            own[piece] += rcv_y[piece].astype(jnp.float32)

        kgrad_ref[piece] = own[piece, 0].astype(jnp.bfloat16)
        vgrad_ref[piece] = own[piece, 1].astype(jnp.bfloat16)

    for piece in range(2):

        @pl.when(y_needed[piece])
        def _(piece=piece):
            fetch_y(piece).wait_send()
            back_y(piece).wait_send()

    def drain(step, carry):
        for piece in range(2):

            @pl.when(has_above & (place - step >= 0))
            def _(piece=piece):
                fetch(UP, piece, step, place, place).wait_send()

            @pl.when(has_below & (place + step < RUN))
            def _(piece=piece):
                fetch(DOWN, piece, step, place, place).wait_send()

            @pl.when(step - (RUN - 1) + place >= 0)
            def _(piece=piece):
                back(DOWN, piece, step, place).wait_send()

            @pl.when(RUN - 1 - step + place < RUN)
            def _(piece=piece):
                back(UP, piece, step, place).wait_send()

        return carry

    lax.fori_loop(0, RUN - 1, drain, 0)


def local(queries, keys, values, out_grad, block_doc):
    runs = lax.axis_size("ctx") // RUN
    bf16, f32 = jnp.bfloat16, jnp.float32
    wide = (2, TOK, COLS)
    thin = (2, TOK, HD)
    any_space = pl.BlockSpec(memory_space=pl.ANY)
    vmem = pl.BlockSpec(memory_space=pltpu.VMEM)
    dma = pltpu.SemaphoreType.DMA
    results = pl.pallas_call(
        functools.partial(kernel, runs),
        out_shape=[
            jax.ShapeDtypeStruct(wide, bf16),
            jax.ShapeDtypeStruct(wide, bf16),
            jax.ShapeDtypeStruct(thin, bf16),
            jax.ShapeDtypeStruct(thin, bf16),
        ],
        in_specs=[pl.BlockSpec(memory_space=pltpu.SMEM)] + [any_space] * 4,
        out_specs=[vmem] * 4,
        scratch_shapes=[
            pltpu.VMEM((2, RUN + 1, 2, TOK, HD), bf16),
            pltpu.VMEM((2, 2, HD, RUN * TOK), bf16),
            pltpu.VMEM((2, COLS, HD), bf16),
            pltpu.VMEM((2, COLS, HD), bf16),
            pltpu.VMEM((2, RUN * TOK, COLS), f32),
            pltpu.VMEM((2, RUN * TOK, COLS), f32),
            pltpu.VMEM((2, 8, COLS), f32),
            pltpu.VMEM((2, RUN * TOK, COLS), bf16),
            pltpu.VMEM((2, RUN * TOK, COLS), bf16),
            pltpu.VMEM((2, 2, 2, TOK, HD), f32),
            pltpu.VMEM((2, 2, TOK, HD), f32),
            pltpu.VMEM((2, RUN, 2, TOK, HD), bf16),
            pltpu.VMEM((2, 2, RUN, 2, TOK, HD), bf16),
            pltpu.VMEM((2, 2, TOK, HD), bf16),
            dma((2, 2)),
            dma((2, 2, GROUP)),
            dma((2, 2, RUN)),
            dma((2, 2, RUN)),
            dma((2,)),
            dma((2,)),
            dma((2, 2, RUN)),
            dma((2, 2, RUN)),
            dma((2,)),
            dma((2,)),
        ],
        compiler_params=pltpu.CompilerParams(
            collective_id=0, has_side_effects=True, vmem_limit_bytes=60 * 1024 * 1024
        ),
    )(
        block_doc,
        queries.reshape(wide),
        keys.reshape(thin),
        values.reshape(thin),
        out_grad.reshape(wide),
    )
    return tuple(array[:, None] for array in results)


def solution(mesh):
    spec = P(None, "ctx", None, "tp")
    return jax.shard_map(
        local,
        mesh=mesh,
        in_specs=(spec, spec, spec, spec, P()),
        out_specs=(spec, spec, spec, spec),
        check_vma=False,
    )
```

```python
import functools
import math

import jax
import jax.numpy as jnp
from jax import lax
from jax.experimental import pallas as pl
from jax.experimental.pallas import tpu as pltpu
from jax.sharding import PartitionSpec as P

HD = 128
GROUP = 8
TOK = 128
RUN = 8
COLS = GROUP * TOK
WIDE = 256
MASKED = -1e30
SCALE = 1.0 / math.sqrt(HD)
EXP2_SCALE = SCALE * math.log2(math.e)
UP, DOWN = 0, 1
VMEM_LIMIT = 44 * 1024 * 1024


def dot(left, right, left_dim, right_dim):
    return lax.dot_general(
        left, right, (((left_dim,), (right_dim,)), ((), ())), preferred_element_type=jnp.float32
    )


def rows_of(slot):
    return pl.ds(pl.multiple_of(slot * TOK, TOK), TOK)


def kernel(
    runs,
    doc_ref,
    q_hbm,
    k_hbm,
    v_hbm,
    g_hbm,
    out_ref,
    qgrad_ref,
    kgrad_ref,
    vgrad_ref,
    kv,
    kv_t,
    queries,
    grads,
    scores,
    dprobs,
    peak,
    probs,
    dscores,
    acc,
    own,
    snd,
    rcv,
    local_sem,
    load_sem,
    fetch_send,
    fetch_recv,
    back_send,
    back_recv,
):
    index = lax.axis_index("ctx")
    run = lax.div(index, RUN)
    place = lax.rem(index, RUN)
    after = lax.rem(run + 1, runs)
    before = lax.rem(run + runs - 1, runs)
    ahead = (1, -1)
    room = (RUN - 1 - place, place)
    trees = ((UP, 0), (DOWN, 1), (UP, 1), (DOWN, 0))
    receivers_run = {(UP, 0): run, (UP, 1): before, (DOWN, 0): after, (DOWN, 1): run}
    owners_run = {(UP, 0): run, (UP, 1): after, (DOWN, 0): before, (DOWN, 1): run}

    def copy(src, dst, send, recv, target):
        return pltpu.make_async_remote_copy(
            src_ref=src,
            dst_ref=dst,
            send_sem=send,
            recv_sem=recv,
            device_id={"ctx": target},
            device_id_type=pl.DeviceIdType.MESH,
        )

    kv_loads = []
    for piece in range(2):
        for part, source in enumerate((k_hbm, v_hbm)):
            kv_loads.append(
                pltpu.make_async_copy(
                    source.at[piece], kv.at[piece, place, part], local_sem.at[piece, part]
                )
            )
    for load in kv_loads:
        load.start()
    loads = []
    for piece in range(2):
        for which, (source, target) in enumerate(((q_hbm, queries), (g_hbm, grads))):
            for head in range(GROUP):
                span = pl.ds(head * TOK, TOK)
                loads.append(
                    pltpu.make_async_copy(
                        source.at[piece, :, span],
                        target.at[piece, span],
                        load_sem.at[piece, which, head],
                    )
                )
    for load in loads:
        load.start()

    barrier = pltpu.get_barrier_semaphore()

    for direction in (UP, DOWN):
        for away in (1, 2):

            @pl.when(room[direction] >= away)
            def _(direction=direction, away=away):
                for at_run in (run, receivers_run[direction, 1 - direction]):
                    pl.semaphore_signal(
                        barrier,
                        inc=1,
                        device_id={"ctx": at_run * RUN + place + ahead[direction] * away},
                        device_id_type=pl.DeviceIdType.MESH,
                    )

    peers = 2 * (jnp.minimum(room[UP], 2) + jnp.minimum(room[DOWN], 2))
    pl.semaphore_wait(barrier, peers)

    for load in kv_loads:
        load.wait()

    def fetch(direction, piece, part, distance, slot, at_run, away):
        return copy(
            kv.at[piece, slot, part],
            kv.at[piece, slot, part],
            fetch_send.at[direction, piece, part, distance],
            fetch_recv.at[direction, piece, part, distance],
            at_run * RUN + place + ahead[direction] * away,
        )

    for away in (2, 1):
        for part in range(2):
            for direction, piece in trees:

                @pl.when(room[direction] >= away)
                def _(direction=direction, piece=piece, part=part, away=away):
                    at_run = receivers_run[direction, piece]
                    fetch(direction, piece, part, away, place, at_run, away).start()

    def doc_of(piece, run_of_slot, slot):
        at = run_of_slot * RUN + slot
        inside = (at >= 0) & (at < runs * RUN)
        at = jnp.clip(at, 0, runs * RUN - 1)
        block = at if piece == 0 else 2 * runs * RUN - 1 - at
        return jnp.where(inside, doc_ref[block], -1)

    my_docs = [doc_of(piece, run, place) for piece in range(2)]
    key_row = lax.broadcasted_iota(jnp.int32, (TOK, WIDE), 0)
    query_row = lax.rem(lax.broadcasted_iota(jnp.int32, (TOK, WIDE), 1), TOK)
    causal = key_row <= query_row

    def visit(slot, is_own):
        for piece in range(2):
            keys = kv[piece, slot, 0]
            vals = kv[piece, slot, 1]
            kv_t[piece, 0, :, rows_of(slot)] = keys.T
            kv_t[piece, 1, :, rows_of(slot)] = vals.T
            if not is_own:
                if piece == 0:
                    run_of_slot = jnp.where(slot > place, run - 1, run)
                else:
                    run_of_slot = jnp.where(slot < place, run + 1, run)
                doc = doc_of(piece, run_of_slot, slot)
                bias = jnp.where(doc == my_docs[piece], 0.0, MASKED)
            for first in range(0, COLS, WIDE):
                cols = pl.ds(first, WIDE)
                block = dot(keys, queries[piece, cols], 1, 1)
                if is_own:
                    block = jnp.where(causal, block, MASKED)
                else:
                    block = block + bias
                scores[piece, rows_of(slot), cols] = block
                top = jnp.max(block.reshape(TOK // 8, 8, WIDE), axis=0)
                if not is_own:
                    top = jnp.maximum(top, peak[piece, :, cols])
                peak[piece, :, cols] = top
                dprobs[piece, rows_of(slot), cols] = dot(vals, grads[piece, cols], 1, 1)

    for load in loads:
        load.wait()
    visit(place, True)

    def slot_at(direction, distance):
        return place - ahead[direction] * distance, room[1 - direction] >= distance

    def fetch_step(step, carry):
        for part in range(2):
            for direction, piece in trees:
                distance = 2 * step + 2
                slot, present = slot_at(direction, distance)

                @pl.when(present)
                def _(direction=direction, piece=piece, part=part, slot=slot, distance=distance):
                    fetch(direction, piece, part, distance, slot, run, 1).wait_recv()
                    for away in (2, 1):

                        @pl.when(room[direction] >= away)
                        def _(away=away):
                            fetch(
                                direction, piece, part, distance + away, slot, run, away
                            ).start()

        for part in range(2):
            for direction, piece in trees:
                distance = 2 * step + 1
                slot, present = slot_at(direction, distance)

                @pl.when(present)
                def _(direction=direction, piece=piece, part=part, slot=slot, distance=distance):
                    fetch(direction, piece, part, distance, slot, run, 1).wait_recv()

        def visit_pair(which, carry):
            for direction in (UP, DOWN):
                slot, present = slot_at(direction, 2 * step + 1 + which)

                @pl.when(present)
                def _(slot=slot):
                    visit(slot, False)

            return carry

        return lax.fori_loop(0, 2, visit_pair, carry)

    lax.fori_loop(0, RUN // 2, fetch_step, 0)

    def soften(group, carry):
        for piece in range(2):
            cols = pl.ds(pl.multiple_of(group * WIDE, WIDE), WIDE)
            top = jnp.max(peak[piece, :, cols], axis=0, keepdims=True)
            total = jnp.zeros((8, WIDE), jnp.float32)
            delta = jnp.zeros((8, WIDE), jnp.float32)
            for slot in range(RUN):
                rows = pl.ds(slot * TOK, TOK)
                weight = jnp.exp2((scores[piece, rows, cols] - top) * EXP2_SCALE)
                scores[piece, rows, cols] = weight
                total += jnp.sum(weight.reshape(TOK // 8, 8, WIDE), axis=0)
                delta += jnp.sum(
                    (weight * dprobs[piece, rows, cols]).reshape(TOK // 8, 8, WIDE), axis=0
                )
            inverse = 1.0 / jnp.sum(total, axis=0, keepdims=True)
            delta = jnp.sum(delta, axis=0, keepdims=True) * inverse
            for slot in range(RUN):
                rows = pl.ds(slot * TOK, TOK)
                prob = scores[piece, rows, cols] * inverse
                probs[piece, rows, cols] = prob.astype(jnp.bfloat16)
                dscores[piece, rows, cols] = (prob * (dprobs[piece, rows, cols] - delta)).astype(
                    jnp.bfloat16
                )
        return carry

    lax.fori_loop(0, COLS // WIDE, soften, 0)

    def key_side(piece, slot):
        rows = rows_of(slot)
        return (
            dot(dscores[piece, rows, :], queries[piece], 1, 0) * SCALE,
            dot(probs[piece, rows, :], grads[piece], 1, 0),
        )

    def back(direction, piece, part, distance, slot, even, owner_is_next):
        at_run = jnp.where(owner_is_next, owners_run[direction, piece], run)
        return copy(
            snd.at[piece, slot, part],
            rcv.at[direction, piece, even, slot, part],
            back_send.at[direction, piece, part, distance],
            back_recv.at[direction, piece, part, distance],
            at_run * RUN + place - ahead[direction] * (1 + even),
        )

    def odd_step(step, carry):
        distance = RUN - 1 - 2 * step
        for direction, piece in trees:
            slot, present = slot_at(direction, distance)

            @pl.when(present)
            def _(direction=direction, piece=piece, slot=slot):
                for part, value in enumerate(key_side(piece, slot)):
                    snd[piece, slot, part] = value.astype(jnp.bfloat16)
                    back(direction, piece, part, distance, slot, 0, distance == 1).start()

        return carry

    lax.fori_loop(0, RUN // 2, odd_step, 0)

    def gather(total, direction, piece, part, distance, slot):
        for even in (0, 1):

            @pl.when(room[direction] > even)
            def _(even=even):
                child = distance + 1 + even
                back(direction, piece, part, child, slot, even, False).wait_recv()
                total[...] += rcv[direction, piece, even, slot, part].astype(jnp.float32)

    def even_step(step, carry):
        distance = RUN - 2 - 2 * step
        for direction, piece in trees:
            slot, present = slot_at(direction, distance)

            @pl.when(present)
            def _(direction=direction, piece=piece, slot=slot):
                for part, value in enumerate(key_side(piece, slot)):
                    acc[direction, piece, part] = value

        for part in range(2):
            for direction, piece in trees:
                slot, present = slot_at(direction, distance)

                @pl.when(present)
                def _(direction=direction, piece=piece, part=part, slot=slot):
                    total = acc.at[direction, piece, part]
                    gather(total, direction, piece, part, distance, slot)
                    snd[piece, slot, part] = total[...].astype(jnp.bfloat16)
                    back(direction, piece, part, distance, slot, 1, distance == 2).start()

        return carry

    lax.fori_loop(0, RUN // 2 - 1, even_step, 0)

    for piece in range(2):
        for part, value in enumerate(key_side(piece, place)):
            own[piece, part] = value

    def query_side(group, carry):
        for piece in range(2):
            cols = pl.ds(pl.multiple_of(group * WIDE, WIDE), WIDE)
            attended = dot(kv_t[piece, 1], probs[piece, :, cols], 1, 0)
            out_ref[piece, :, cols] = jnp.concatenate(
                [attended[:, :TOK].T, attended[:, TOK:].T], axis=1
            ).astype(jnp.bfloat16)
            pulled = dot(kv_t[piece, 0], dscores[piece, :, cols], 1, 0) * SCALE
            qgrad_ref[piece, :, cols] = jnp.concatenate(
                [pulled[:, :TOK].T, pulled[:, TOK:].T], axis=1
            ).astype(jnp.bfloat16)
        return carry

    lax.fori_loop(0, COLS // WIDE, query_side, 0)

    for part in range(2):
        for direction, piece in trees:
            gather(own.at[piece, part], direction, piece, part, 0, place)

    for piece in range(2):
        kgrad_ref[piece] = own[piece, 0].astype(jnp.bfloat16)
        vgrad_ref[piece] = own[piece, 1].astype(jnp.bfloat16)

    def drain(step, carry):
        distance = step + 1
        away = 1 + lax.rem(step, 2)
        for direction, piece in trees:
            for part in range(2):

                @pl.when((room[1 - direction] >= distance - away) & (room[direction] >= away))
                def _(direction=direction, piece=piece, part=part):
                    fetch(direction, piece, part, distance, place, run, 1).wait_send()

                @pl.when(room[1 - direction] >= distance)
                def _(direction=direction, piece=piece, part=part):
                    back(direction, piece, part, distance, place, 0, False).wait_send()

        return carry

    lax.fori_loop(0, RUN - 1, drain, 0)


def local(queries, keys, values, out_grad, block_doc):
    runs = lax.axis_size("ctx") // RUN
    bf16, f32 = jnp.bfloat16, jnp.float32
    wide = (2, TOK, COLS)
    thin = (2, TOK, HD)
    any_space = pl.BlockSpec(memory_space=pltpu.HBM)
    vmem = pl.BlockSpec(memory_space=pltpu.VMEM)
    dma = pltpu.SemaphoreType.DMA
    results = pl.pallas_call(
        functools.partial(kernel, runs),
        out_shape=[
            jax.ShapeDtypeStruct(wide, bf16),
            jax.ShapeDtypeStruct(wide, bf16),
            jax.ShapeDtypeStruct(thin, bf16),
            jax.ShapeDtypeStruct(thin, bf16),
        ],
        in_specs=[pl.BlockSpec(memory_space=pltpu.SMEM)] + [any_space] * 4,
        out_specs=[vmem] * 4,
        scratch_shapes=[
            pltpu.VMEM((2, RUN, 2, TOK, HD), bf16),
            pltpu.VMEM((2, 2, HD, RUN * TOK), bf16),
            pltpu.VMEM((2, COLS, HD), bf16),
            pltpu.VMEM((2, COLS, HD), bf16),
            pltpu.VMEM((2, RUN * TOK, COLS), f32),
            pltpu.VMEM((2, RUN * TOK, COLS), f32),
            pltpu.VMEM((2, 8, COLS), f32),
            pltpu.VMEM((2, RUN * TOK, COLS), bf16),
            pltpu.VMEM((2, RUN * TOK, COLS), bf16),
            pltpu.VMEM((2, 2, 2, TOK, HD), f32),
            pltpu.VMEM((2, 2, TOK, HD), f32),
            pltpu.VMEM((2, RUN, 2, TOK, HD), bf16),
            pltpu.VMEM((2, 2, 2, RUN, 2, TOK, HD), bf16),
            dma((2, 2)),
            dma((2, 2, GROUP)),
            dma((2, 2, 2, RUN)),
            dma((2, 2, 2, RUN)),
            dma((2, 2, 2, RUN)),
            dma((2, 2, 2, RUN)),
        ],
        compiler_params=pltpu.CompilerParams(
            collective_id=0, has_side_effects=True, vmem_limit_bytes=VMEM_LIMIT
        ),
    )(
        block_doc,
        queries.reshape(wide),
        keys.reshape(thin),
        values.reshape(thin),
        out_grad.reshape(wide),
    )
    return tuple(array[:, None] for array in results)


def solution(mesh):
    spec = P(None, "ctx", None, "tp")
    return jax.shard_map(
        local,
        mesh=mesh,
        in_specs=(spec, spec, spec, spec, P()),
        out_specs=(spec, spec, spec, spec),
        check_vma=False,
    )
```

```python
import functools
import math

import jax
import jax.numpy as jnp
from jax import lax
from jax.experimental import pallas as pl
from jax.experimental.pallas import tpu as pltpu
from jax.sharding import PartitionSpec as P

HD = 128
GROUP = 8
TOK = 128
RUN = 8
COLS = GROUP * TOK
WIDE = 256
MASKED = -1e30
SCALE = 1.0 / math.sqrt(HD)
EXP2_SCALE = SCALE * math.log2(math.e)
UP, DOWN = 0, 1
LAG = 2
VMEM_LIMIT = 44 * 1024 * 1024


def dot(left, right, left_dim, right_dim):
    return lax.dot_general(
        left, right, (((left_dim,), (right_dim,)), ((), ())), preferred_element_type=jnp.float32
    )


def rows_of(slot):
    return pl.ds(pl.multiple_of(slot * TOK, TOK), TOK)


def kernel(
    runs,
    doc_ref,
    q_hbm,
    k_hbm,
    v_hbm,
    g_hbm,
    out_ref,
    qgrad_ref,
    kgrad_ref,
    vgrad_ref,
    kv,
    kv_t,
    queries,
    grads,
    scores,
    dprobs,
    peak,
    probs,
    dscores,
    acc,
    own,
    snd,
    rcv,
    local_sem,
    load_sem,
    fetch_send,
    fetch_recv,
    back_send,
    back_recv,
):
    index = lax.axis_index("ctx")
    run = lax.div(index, RUN)
    place = lax.rem(index, RUN)
    after = lax.rem(run + 1, runs)
    before = lax.rem(run + runs - 1, runs)
    ahead = (1, -1)
    room = (RUN - 1 - place, place)
    trees = ((UP, 0), (DOWN, 1), (UP, 1), (DOWN, 0))
    receivers_run = {(UP, 0): run, (UP, 1): before, (DOWN, 0): after, (DOWN, 1): run}
    owners_run = {(UP, 0): run, (UP, 1): after, (DOWN, 0): before, (DOWN, 1): run}

    def copy(src, dst, send, recv, target):
        return pltpu.make_async_remote_copy(
            src_ref=src,
            dst_ref=dst,
            send_sem=send,
            recv_sem=recv,
            device_id={"ctx": target},
            device_id_type=pl.DeviceIdType.MESH,
        )

    kv_loads = []
    for piece in range(2):
        for part, source in enumerate((k_hbm, v_hbm)):
            kv_loads.append(
                pltpu.make_async_copy(
                    source.at[piece], kv.at[piece, place, part], local_sem.at[piece, part]
                )
            )
    for load in kv_loads:
        load.start()
    loads = []
    for piece in range(2):
        for which, (source, target) in enumerate(((q_hbm, queries), (g_hbm, grads))):
            for head in range(GROUP):
                span = pl.ds(head * TOK, TOK)
                loads.append(
                    pltpu.make_async_copy(
                        source.at[piece, :, span],
                        target.at[piece, span],
                        load_sem.at[piece, which, head],
                    )
                )
    for load in loads:
        load.start()

    barrier = pltpu.get_barrier_semaphore()

    for direction in (UP, DOWN):
        for away in (1, 2):

            @pl.when(room[direction] >= away)
            def _(direction=direction, away=away):
                for at_run in (run, receivers_run[direction, 1 - direction]):
                    pl.semaphore_signal(
                        barrier,
                        inc=1,
                        device_id={"ctx": at_run * RUN + place + ahead[direction] * away},
                        device_id_type=pl.DeviceIdType.MESH,
                    )

    peers = 2 * (jnp.minimum(room[UP], 2) + jnp.minimum(room[DOWN], 2))
    pl.semaphore_wait(barrier, peers)

    for load in kv_loads:
        load.wait()

    def fetch(direction, piece, part, distance, slot, at_run, away):
        return copy(
            kv.at[piece, slot, part],
            kv.at[piece, slot, part],
            fetch_send.at[direction, piece, part, distance],
            fetch_recv.at[direction, piece, part, distance],
            at_run * RUN + place + ahead[direction] * away,
        )

    def send_own(piece):
        for away in (2, 1):
            for part in range(2):
                for direction in (UP, DOWN):

                    @pl.when(room[direction] >= away)
                    def _(direction=direction, part=part, away=away):
                        at_run = receivers_run[direction, piece]
                        fetch(direction, piece, part, away, place, at_run, away).start()

    send_own(0)

    def doc_of(piece, run_of_slot, slot):
        at = run_of_slot * RUN + slot
        inside = (at >= 0) & (at < runs * RUN)
        at = jnp.clip(at, 0, runs * RUN - 1)
        block = at if piece == 0 else 2 * runs * RUN - 1 - at
        return jnp.where(inside, doc_ref[block], -1)

    my_docs = [doc_of(piece, run, place) for piece in range(2)]
    key_row = lax.broadcasted_iota(jnp.int32, (TOK, WIDE), 0)
    query_row = lax.rem(lax.broadcasted_iota(jnp.int32, (TOK, WIDE), 1), TOK)
    causal = key_row <= query_row

    def visit(piece, slot, is_own):
        keys = kv[piece, slot, 0]
        vals = kv[piece, slot, 1]
        kv_t[piece, 0, :, rows_of(slot)] = keys.T
        kv_t[piece, 1, :, rows_of(slot)] = vals.T
        if not is_own:
            if piece == 0:
                run_of_slot = jnp.where(slot > place, run - 1, run)
            else:
                run_of_slot = jnp.where(slot < place, run + 1, run)
            doc = doc_of(piece, run_of_slot, slot)
            bias = jnp.where(doc == my_docs[piece], 0.0, MASKED)
        for first in range(0, COLS, WIDE):
            cols = pl.ds(first, WIDE)
            block = dot(keys, queries[piece, cols], 1, 1)
            if is_own:
                block = jnp.where(causal, block, MASKED)
            else:
                block = block + bias
            scores[piece, rows_of(slot), cols] = block
            top = jnp.max(block.reshape(TOK // 8, 8, WIDE), axis=0)
            if not is_own:
                top = jnp.maximum(top, peak[piece, :, cols])
            peak[piece, :, cols] = top
            dprobs[piece, rows_of(slot), cols] = dot(vals, grads[piece, cols], 1, 1)

    for load in loads:
        load.wait()
    for piece in range(2):
        visit(piece, place, True)

    def slot_at(direction, distance):
        return place - ahead[direction] * distance, room[1 - direction] >= distance

    def fetch_step(piece, step):
        for even in (1, 0):
            distance = 2 * step + 1 + even
            for part in range(2):
                for direction in (UP, DOWN):
                    slot, present = slot_at(direction, distance)

                    @pl.when(present)
                    def _(direction=direction, part=part, slot=slot, distance=distance, even=even):
                        fetch(direction, piece, part, distance, slot, run, 1).wait_recv()
                        if not even:
                            return
                        for away in (2, 1):

                            @pl.when(room[direction] >= away)
                            def _(away=away):
                                fetch(
                                    direction, piece, part, distance + away, slot, run, away
                                ).start()

        def visit_pair(which, carry):
            for direction in (UP, DOWN):
                slot, present = slot_at(direction, 2 * step + 1 + which)

                @pl.when(present)
                def _(slot=slot):
                    visit(piece, slot, False)

            return carry

        lax.fori_loop(0, 2, visit_pair, 0)

    def soften(piece, group):
        cols = pl.ds(pl.multiple_of(group * WIDE, WIDE), WIDE)
        top = jnp.max(peak[piece, :, cols], axis=0, keepdims=True)
        total = jnp.zeros((8, WIDE), jnp.float32)
        delta = jnp.zeros((8, WIDE), jnp.float32)
        for slot in range(RUN):
            rows = pl.ds(slot * TOK, TOK)
            weight = jnp.exp2((scores[piece, rows, cols] - top) * EXP2_SCALE)
            scores[piece, rows, cols] = weight
            total += jnp.sum(weight.reshape(TOK // 8, 8, WIDE), axis=0)
            delta += jnp.sum(
                (weight * dprobs[piece, rows, cols]).reshape(TOK // 8, 8, WIDE), axis=0
            )
        inverse = 1.0 / jnp.sum(total, axis=0, keepdims=True)
        delta = jnp.sum(delta, axis=0, keepdims=True) * inverse
        for slot in range(RUN):
            rows = pl.ds(slot * TOK, TOK)
            prob = scores[piece, rows, cols] * inverse
            probs[piece, rows, cols] = prob.astype(jnp.bfloat16)
            dscores[piece, rows, cols] = (prob * (dprobs[piece, rows, cols] - delta)).astype(
                jnp.bfloat16
            )

    def key_side(piece, slot):
        rows = rows_of(slot)
        return (
            dot(dscores[piece, rows, :], queries[piece], 1, 0) * SCALE,
            dot(probs[piece, rows, :], grads[piece], 1, 0),
        )

    def back(direction, piece, part, distance, slot, even, owner_is_next):
        at_run = jnp.where(owner_is_next, owners_run[direction, piece], run)
        return copy(
            snd.at[piece, slot, part],
            rcv.at[direction, piece, even, slot, part],
            back_send.at[direction, piece, part, distance],
            back_recv.at[direction, piece, part, distance],
            at_run * RUN + place - ahead[direction] * (1 + even),
        )

    def odd_step(piece, step):
        distance = RUN - 1 - 2 * step
        for direction in (UP, DOWN):
            slot, present = slot_at(direction, distance)

            @pl.when(present)
            def _(direction=direction, slot=slot):
                for part, value in enumerate(key_side(piece, slot)):
                    snd[piece, slot, part] = value.astype(jnp.bfloat16)
                    back(direction, piece, part, distance, slot, 0, distance == 1).start()

    def gather(total, direction, piece, part, distance, slot):
        for even in (0, 1):

            @pl.when(room[direction] > even)
            def _(even=even):
                child = distance + 1 + even
                back(direction, piece, part, child, slot, even, False).wait_recv()
                total[...] += rcv[direction, piece, even, slot, part].astype(jnp.float32)

    def even_step(piece, step):
        distance = RUN - 2 - 2 * step
        for direction in (UP, DOWN):
            slot, present = slot_at(direction, distance)

            @pl.when(present)
            def _(direction=direction, slot=slot):
                for part, value in enumerate(key_side(piece, slot)):
                    acc[direction, piece, part] = value

        for part in range(2):
            for direction in (UP, DOWN):
                slot, present = slot_at(direction, distance)

                @pl.when(present)
                def _(direction=direction, part=part, slot=slot):
                    total = acc.at[direction, piece, part]
                    gather(total, direction, piece, part, distance, slot)
                    snd[piece, slot, part] = total[...].astype(jnp.bfloat16)
                    back(direction, piece, part, distance, slot, 1, distance == 2).start()

    def query_side(piece, group):
        cols = pl.ds(pl.multiple_of(group * WIDE, WIDE), WIDE)
        attended = dot(kv_t[piece, 1], probs[piece, :, cols], 1, 0)
        out_ref[piece, :, cols] = jnp.concatenate(
            [attended[:, :TOK].T, attended[:, TOK:].T], axis=1
        ).astype(jnp.bfloat16)
        pulled = dot(kv_t[piece, 0], dscores[piece, :, cols], 1, 0) * SCALE
        qgrad_ref[piece, :, cols] = jnp.concatenate(
            [pulled[:, :TOK].T, pulled[:, TOK:].T], axis=1
        ).astype(jnp.bfloat16)

    def finish(piece):
        for part, value in enumerate(key_side(piece, place)):
            own[piece, part] = value
        repeat(COLS // WIDE, query_side, piece)
        for part in range(2):
            for direction in (UP, DOWN):
                gather(own.at[piece, part], direction, piece, part, 0, place)
        kgrad_ref[piece] = own[piece, 0].astype(jnp.bfloat16)
        vgrad_ref[piece] = own[piece, 1].astype(jnp.bfloat16)

    def repeat(count, action, piece):
        def body(step, carry):
            action(piece, step)
            return carry

        lax.fori_loop(0, count, body, 0)

    def stage(time, carry):
        for piece in range(2):
            now = time - LAG * piece
            if piece == 1:

                @pl.when(now == -1)
                def _():
                    send_own(1)

            @pl.when((now >= 0) & (now < RUN // 2))
            def _(piece=piece, now=now):
                fetch_step(piece, now)

            @pl.when(now == RUN // 2 - 1)
            def _(piece=piece):
                repeat(COLS // WIDE, soften, piece)
                repeat(RUN // 2, odd_step, piece)

            @pl.when((now >= RUN // 2) & (now < RUN - 1))
            def _(piece=piece, now=now):
                even_step(piece, now - RUN // 2)

            @pl.when(now == RUN - 1)
            def _(piece=piece):
                finish(piece)

        return carry

    lax.fori_loop(0, RUN + LAG, stage, 0)

    def drain(step, carry):
        distance = step + 1
        away = 1 + lax.rem(step, 2)
        for direction, piece in trees:
            for part in range(2):

                @pl.when((room[1 - direction] >= distance - away) & (room[direction] >= away))
                def _(direction=direction, piece=piece, part=part):
                    fetch(direction, piece, part, distance, place, run, 1).wait_send()

                @pl.when(room[1 - direction] >= distance)
                def _(direction=direction, piece=piece, part=part):
                    back(direction, piece, part, distance, place, 0, False).wait_send()

        return carry

    lax.fori_loop(0, RUN - 1, drain, 0)


def local(queries, keys, values, out_grad, block_doc):
    runs = lax.axis_size("ctx") // RUN
    bf16, f32 = jnp.bfloat16, jnp.float32
    wide = (2, TOK, COLS)
    thin = (2, TOK, HD)
    any_space = pl.BlockSpec(memory_space=pltpu.HBM)
    vmem = pl.BlockSpec(memory_space=pltpu.VMEM)
    dma = pltpu.SemaphoreType.DMA
    results = pl.pallas_call(
        functools.partial(kernel, runs),
        out_shape=[
            jax.ShapeDtypeStruct(wide, bf16),
            jax.ShapeDtypeStruct(wide, bf16),
            jax.ShapeDtypeStruct(thin, bf16),
            jax.ShapeDtypeStruct(thin, bf16),
        ],
        in_specs=[pl.BlockSpec(memory_space=pltpu.SMEM)] + [any_space] * 4,
        out_specs=[vmem] * 4,
        scratch_shapes=[
            pltpu.VMEM((2, RUN, 2, TOK, HD), bf16),
            pltpu.VMEM((2, 2, HD, RUN * TOK), bf16),
            pltpu.VMEM((2, COLS, HD), bf16),
            pltpu.VMEM((2, COLS, HD), bf16),
            pltpu.VMEM((2, RUN * TOK, COLS), f32),
            pltpu.VMEM((2, RUN * TOK, COLS), f32),
            pltpu.VMEM((2, 8, COLS), f32),
            pltpu.VMEM((2, RUN * TOK, COLS), bf16),
            pltpu.VMEM((2, RUN * TOK, COLS), bf16),
            pltpu.VMEM((2, 2, 2, TOK, HD), f32),
            pltpu.VMEM((2, 2, TOK, HD), f32),
            pltpu.VMEM((2, RUN, 2, TOK, HD), bf16),
            pltpu.VMEM((2, 2, 2, RUN, 2, TOK, HD), bf16),
            dma((2, 2)),
            dma((2, 2, GROUP)),
            dma((2, 2, 2, RUN)),
            dma((2, 2, 2, RUN)),
            dma((2, 2, 2, RUN)),
            dma((2, 2, 2, RUN)),
        ],
        compiler_params=pltpu.CompilerParams(
            collective_id=0, has_side_effects=True, vmem_limit_bytes=VMEM_LIMIT
        ),
    )(
        block_doc,
        queries.reshape(wide),
        keys.reshape(thin),
        values.reshape(thin),
        out_grad.reshape(wide),
    )
    return tuple(array[:, None] for array in results)


def solution(mesh):
    spec = P(None, "ctx", None, "tp")
    return jax.shard_map(
        local,
        mesh=mesh,
        in_specs=(spec, spec, spec, spec, P()),
        out_specs=(spec, spec, spec, spec),
        check_vma=False,
    )
```

```python
import functools
import math

import jax
import jax.numpy as jnp
from jax import lax
from jax.experimental import pallas as pl
from jax.experimental.pallas import tpu as pltpu
from jax.sharding import PartitionSpec as P

HD = 128
GROUP = 8
TOK = 128
RUN = 8
COLS = GROUP * TOK
WIDE = 256
MASKED = -1e30
SCALE = 1.0 / math.sqrt(HD)
EXP2_SCALE = SCALE * math.log2(math.e)
UP, DOWN = 0, 1
LAG = 4
VMEM_LIMIT = 44 * 1024 * 1024


def dot(left, right, left_dim, right_dim):
    return lax.dot_general(
        left, right, (((left_dim,), (right_dim,)), ((), ())), preferred_element_type=jnp.float32
    )


def rows_of(slot):
    return pl.ds(pl.multiple_of(slot * TOK, TOK), TOK)


def kernel(
    runs,
    doc_ref,
    q_hbm,
    k_hbm,
    v_hbm,
    g_hbm,
    out_ref,
    qgrad_ref,
    kgrad_ref,
    vgrad_ref,
    kv,
    kv_t,
    queries,
    grads,
    scores,
    dprobs,
    peak,
    probs,
    dscores,
    acc,
    own,
    snd,
    rcv,
    local_sem,
    load_sem,
    fetch_send,
    fetch_recv,
    back_send,
    back_recv,
):
    index = lax.axis_index("ctx")
    run = lax.div(index, RUN)
    place = lax.rem(index, RUN)
    after = lax.rem(run + 1, runs)
    before = lax.rem(run + runs - 1, runs)
    ahead = (1, -1)
    room = (RUN - 1 - place, place)
    trees = ((UP, 0), (DOWN, 1), (UP, 1), (DOWN, 0))
    receivers_run = {(UP, 0): run, (UP, 1): before, (DOWN, 0): after, (DOWN, 1): run}
    owners_run = {(UP, 0): run, (UP, 1): after, (DOWN, 0): before, (DOWN, 1): run}

    def copy(src, dst, send, recv, target):
        return pltpu.make_async_remote_copy(
            src_ref=src,
            dst_ref=dst,
            send_sem=send,
            recv_sem=recv,
            device_id={"ctx": target},
            device_id_type=pl.DeviceIdType.MESH,
        )

    kv_loads = []
    for piece in range(2):
        for part, source in enumerate((k_hbm, v_hbm)):
            kv_loads.append(
                pltpu.make_async_copy(
                    source.at[piece], kv.at[piece, place, part], local_sem.at[piece, part]
                )
            )
    for load in kv_loads:
        load.start()
    loads = []
    for piece in range(2):
        for which, (source, target) in enumerate(((q_hbm, queries), (g_hbm, grads))):
            for head in range(GROUP):
                span = pl.ds(head * TOK, TOK)
                loads.append(
                    pltpu.make_async_copy(
                        source.at[piece, :, span],
                        target.at[piece, span],
                        load_sem.at[piece, which, head],
                    )
                )
    for load in loads:
        load.start()

    barrier = pltpu.get_barrier_semaphore()

    for direction in (UP, DOWN):
        for away in (1, 2):

            @pl.when(room[direction] >= away)
            def _(direction=direction, away=away):
                for at_run in (run, receivers_run[direction, 1 - direction]):
                    pl.semaphore_signal(
                        barrier,
                        inc=1,
                        device_id={"ctx": at_run * RUN + place + ahead[direction] * away},
                        device_id_type=pl.DeviceIdType.MESH,
                    )

    peers = 2 * (jnp.minimum(room[UP], 2) + jnp.minimum(room[DOWN], 2))
    pl.semaphore_wait(barrier, peers)

    for load in kv_loads:
        load.wait()

    def fetch(direction, piece, part, distance, slot, at_run, away):
        return copy(
            kv.at[piece, slot, part],
            kv.at[piece, slot, part],
            fetch_send.at[direction, piece, part, distance],
            fetch_recv.at[direction, piece, part, distance],
            at_run * RUN + place + ahead[direction] * away,
        )

    def send_own(piece):
        for away in (2, 1):
            for part in range(2):
                for direction in (UP, DOWN):

                    @pl.when(room[direction] >= away)
                    def _(direction=direction, part=part, away=away):
                        at_run = receivers_run[direction, piece]
                        fetch(direction, piece, part, away, place, at_run, away).start()

    send_own(0)

    def doc_of(piece, run_of_slot, slot):
        at = run_of_slot * RUN + slot
        inside = (at >= 0) & (at < runs * RUN)
        at = jnp.clip(at, 0, runs * RUN - 1)
        block = at if piece == 0 else 2 * runs * RUN - 1 - at
        return jnp.where(inside, doc_ref[block], -1)

    my_docs = [doc_of(piece, run, place) for piece in range(2)]
    key_row = lax.broadcasted_iota(jnp.int32, (TOK, WIDE), 0)
    query_row = lax.rem(lax.broadcasted_iota(jnp.int32, (TOK, WIDE), 1), TOK)
    causal = key_row <= query_row

    def visit(piece, slot, is_own):
        keys = kv[piece, slot, 0]
        vals = kv[piece, slot, 1]
        kv_t[piece, 0, :, rows_of(slot)] = keys.T
        kv_t[piece, 1, :, rows_of(slot)] = vals.T
        if not is_own:
            if piece == 0:
                run_of_slot = jnp.where(slot > place, run - 1, run)
            else:
                run_of_slot = jnp.where(slot < place, run + 1, run)
            doc = doc_of(piece, run_of_slot, slot)
            bias = jnp.where(doc == my_docs[piece], 0.0, MASKED)
        for first in range(0, COLS, WIDE):
            cols = pl.ds(first, WIDE)
            block = dot(keys, queries[piece, cols], 1, 1)
            if is_own:
                block = jnp.where(causal, block, MASKED)
            else:
                block = block + bias
            scores[piece, rows_of(slot), cols] = block
            top = jnp.max(block.reshape(TOK // 8, 8, WIDE), axis=0)
            if not is_own:
                top = jnp.maximum(top, peak[piece, :, cols])
            peak[piece, :, cols] = top
            dprobs[piece, rows_of(slot), cols] = dot(vals, grads[piece, cols], 1, 1)

    for load in loads:
        load.wait()
    for piece in range(2):
        visit(piece, place, True)

    def slot_at(direction, distance):
        return place - ahead[direction] * distance, room[1 - direction] >= distance

    def fetch_step(piece, step):
        for even in (1, 0):
            distance = 2 * step + 1 + even
            for part in range(2):
                for direction in (UP, DOWN):
                    slot, present = slot_at(direction, distance)

                    @pl.when(present)
                    def _(direction=direction, part=part, slot=slot, distance=distance, even=even):
                        fetch(direction, piece, part, distance, slot, run, 1).wait_recv()
                        if not even:
                            return
                        for away in (2, 1):

                            @pl.when(room[direction] >= away)
                            def _(away=away):
                                fetch(
                                    direction, piece, part, distance + away, slot, run, away
                                ).start()

        def visit_pair(which, carry):
            for direction in (UP, DOWN):
                slot, present = slot_at(direction, 2 * step + 1 + which)

                @pl.when(present)
                def _(slot=slot):
                    visit(piece, slot, False)

            return carry

        lax.fori_loop(0, 2, visit_pair, 0)

    def soften(piece, group):
        cols = pl.ds(pl.multiple_of(group * WIDE, WIDE), WIDE)
        top = jnp.max(peak[piece, :, cols], axis=0, keepdims=True)
        total = jnp.zeros((8, WIDE), jnp.float32)
        delta = jnp.zeros((8, WIDE), jnp.float32)
        for slot in range(RUN):
            rows = pl.ds(slot * TOK, TOK)
            weight = jnp.exp2((scores[piece, rows, cols] - top) * EXP2_SCALE)
            scores[piece, rows, cols] = weight
            total += jnp.sum(weight.reshape(TOK // 8, 8, WIDE), axis=0)
            delta += jnp.sum(
                (weight * dprobs[piece, rows, cols]).reshape(TOK // 8, 8, WIDE), axis=0
            )
        inverse = 1.0 / jnp.sum(total, axis=0, keepdims=True)
        delta = jnp.sum(delta, axis=0, keepdims=True) * inverse
        for slot in range(RUN):
            rows = pl.ds(slot * TOK, TOK)
            prob = scores[piece, rows, cols] * inverse
            probs[piece, rows, cols] = prob.astype(jnp.bfloat16)
            dscores[piece, rows, cols] = (prob * (dprobs[piece, rows, cols] - delta)).astype(
                jnp.bfloat16
            )

    def key_side(piece, slot):
        rows = rows_of(slot)
        return (
            dot(dscores[piece, rows, :], queries[piece], 1, 0) * SCALE,
            dot(probs[piece, rows, :], grads[piece], 1, 0),
        )

    def back(direction, piece, part, distance, slot, even, owner_is_next):
        at_run = jnp.where(owner_is_next, owners_run[direction, piece], run)
        return copy(
            snd.at[piece, slot, part],
            rcv.at[direction, piece, even, slot, part],
            back_send.at[direction, piece, part, distance],
            back_recv.at[direction, piece, part, distance],
            at_run * RUN + place - ahead[direction] * (1 + even),
        )

    def odd_step(piece, step):
        distance = RUN - 1 - 2 * step
        for direction in (UP, DOWN):
            slot, present = slot_at(direction, distance)

            @pl.when(present)
            def _(direction=direction, slot=slot):
                for part, value in enumerate(key_side(piece, slot)):
                    snd[piece, slot, part] = value.astype(jnp.bfloat16)
                    back(direction, piece, part, distance, slot, 0, distance == 1).start()

    def gather(total, direction, piece, part, distance, slot):
        for even in (0, 1):

            @pl.when(room[direction] > even)
            def _(even=even):
                child = distance + 1 + even
                back(direction, piece, part, child, slot, even, False).wait_recv()
                total[...] += rcv[direction, piece, even, slot, part].astype(jnp.float32)

    def even_step(piece, step):
        distance = RUN - 2 - 2 * step
        for direction in (UP, DOWN):
            slot, present = slot_at(direction, distance)

            @pl.when(present)
            def _(direction=direction, slot=slot):
                for part, value in enumerate(key_side(piece, slot)):
                    acc[direction, piece, part] = value

        for part in range(2):
            for direction in (UP, DOWN):
                slot, present = slot_at(direction, distance)

                @pl.when(present)
                def _(direction=direction, part=part, slot=slot):
                    total = acc.at[direction, piece, part]
                    gather(total, direction, piece, part, distance, slot)
                    snd[piece, slot, part] = total[...].astype(jnp.bfloat16)
                    back(direction, piece, part, distance, slot, 1, distance == 2).start()

    def query_side(piece, group):
        cols = pl.ds(pl.multiple_of(group * WIDE, WIDE), WIDE)
        attended = dot(kv_t[piece, 1], probs[piece, :, cols], 1, 0)
        out_ref[piece, :, cols] = jnp.concatenate(
            [attended[:, :TOK].T, attended[:, TOK:].T], axis=1
        ).astype(jnp.bfloat16)
        pulled = dot(kv_t[piece, 0], dscores[piece, :, cols], 1, 0) * SCALE
        qgrad_ref[piece, :, cols] = jnp.concatenate(
            [pulled[:, :TOK].T, pulled[:, TOK:].T], axis=1
        ).astype(jnp.bfloat16)

    def finish(piece):
        for part, value in enumerate(key_side(piece, place)):
            own[piece, part] = value
        repeat(COLS // WIDE, query_side, piece)
        for part in range(2):
            for direction in (UP, DOWN):
                gather(own.at[piece, part], direction, piece, part, 0, place)
        kgrad_ref[piece] = own[piece, 0].astype(jnp.bfloat16)
        vgrad_ref[piece] = own[piece, 1].astype(jnp.bfloat16)

    def repeat(count, action, piece):
        def body(step, carry):
            action(piece, step)
            return carry

        lax.fori_loop(0, count, body, 0)

    def stage(time, carry):
        @pl.when(time == LAG - 1)
        def _():
            send_own(1)

        for piece in range(2):
            now = time - LAG * piece
            @pl.when((now >= 0) & (now < RUN // 2))
            def _(piece=piece, now=now):
                fetch_step(piece, now)

            @pl.when(now == RUN // 2 - 1)
            def _(piece=piece):
                repeat(COLS // WIDE, soften, piece)
                repeat(RUN // 2, odd_step, piece)

            @pl.when((now >= RUN // 2) & (now < RUN - 1))
            def _(piece=piece, now=now):
                even_step(piece, now - RUN // 2)

            @pl.when(now == RUN - 1)
            def _(piece=piece):
                finish(piece)

        return carry

    lax.fori_loop(0, RUN + LAG, stage, 0)

    def drain(step, carry):
        distance = step + 1
        away = 1 + lax.rem(step, 2)
        for direction, piece in trees:
            for part in range(2):

                @pl.when((room[1 - direction] >= distance - away) & (room[direction] >= away))
                def _(direction=direction, piece=piece, part=part):
                    fetch(direction, piece, part, distance, place, run, 1).wait_send()

                @pl.when(room[1 - direction] >= distance)
                def _(direction=direction, piece=piece, part=part):
                    back(direction, piece, part, distance, place, 0, False).wait_send()

        return carry

    lax.fori_loop(0, RUN - 1, drain, 0)


def local(queries, keys, values, out_grad, block_doc):
    runs = lax.axis_size("ctx") // RUN
    bf16, f32 = jnp.bfloat16, jnp.float32
    wide = (2, TOK, COLS)
    thin = (2, TOK, HD)
    any_space = pl.BlockSpec(memory_space=pltpu.HBM)
    vmem = pl.BlockSpec(memory_space=pltpu.VMEM)
    dma = pltpu.SemaphoreType.DMA
    results = pl.pallas_call(
        functools.partial(kernel, runs),
        out_shape=[
            jax.ShapeDtypeStruct(wide, bf16),
            jax.ShapeDtypeStruct(wide, bf16),
            jax.ShapeDtypeStruct(thin, bf16),
            jax.ShapeDtypeStruct(thin, bf16),
        ],
        in_specs=[pl.BlockSpec(memory_space=pltpu.SMEM)] + [any_space] * 4,
        out_specs=[vmem] * 4,
        scratch_shapes=[
            pltpu.VMEM((2, RUN, 2, TOK, HD), bf16),
            pltpu.VMEM((2, 2, HD, RUN * TOK), bf16),
            pltpu.VMEM((2, COLS, HD), bf16),
            pltpu.VMEM((2, COLS, HD), bf16),
            pltpu.VMEM((2, RUN * TOK, COLS), f32),
            pltpu.VMEM((2, RUN * TOK, COLS), f32),
            pltpu.VMEM((2, 8, COLS), f32),
            pltpu.VMEM((2, RUN * TOK, COLS), bf16),
            pltpu.VMEM((2, RUN * TOK, COLS), bf16),
            pltpu.VMEM((2, 2, 2, TOK, HD), f32),
            pltpu.VMEM((2, 2, TOK, HD), f32),
            pltpu.VMEM((2, RUN, 2, TOK, HD), bf16),
            pltpu.VMEM((2, 2, 2, RUN, 2, TOK, HD), bf16),
            dma((2, 2)),
            dma((2, 2, GROUP)),
            dma((2, 2, 2, RUN)),
            dma((2, 2, 2, RUN)),
            dma((2, 2, 2, RUN)),
            dma((2, 2, 2, RUN)),
        ],
        compiler_params=pltpu.CompilerParams(
            collective_id=0, has_side_effects=True, vmem_limit_bytes=VMEM_LIMIT
        ),
    )(
        block_doc,
        queries.reshape(wide),
        keys.reshape(thin),
        values.reshape(thin),
        out_grad.reshape(wide),
    )
    return tuple(array[:, None] for array in results)


def solution(mesh):
    spec = P(None, "ctx", None, "tp")
    return jax.shard_map(
        local,
        mesh=mesh,
        in_specs=(spec, spec, spec, spec, P()),
        out_specs=(spec, spec, spec, spec),
        check_vma=False,
    )
```

```python
import functools
import math

import jax
import jax.numpy as jnp
from jax import lax
from jax.experimental import pallas as pl
from jax.experimental.pallas import tpu as pltpu
from jax.sharding import PartitionSpec as P

HD = 128
GROUP = 8
TOK = 128
RUN = 8
COLS = GROUP * TOK
WIDE = 256
MASKED = -1e30
SCALE = 1.0 / math.sqrt(HD)
EXP2_SCALE = SCALE * math.log2(math.e)
UP, DOWN = 0, 1
LAG = 1
VMEM_LIMIT = 44 * 1024 * 1024


def dot(left, right, left_dim, right_dim):
    return lax.dot_general(
        left, right, (((left_dim,), (right_dim,)), ((), ())), preferred_element_type=jnp.float32
    )


def rows_of(slot):
    return pl.ds(pl.multiple_of(slot * TOK, TOK), TOK)


def kernel(
    runs,
    doc_ref,
    q_hbm,
    k_hbm,
    v_hbm,
    g_hbm,
    out_ref,
    qgrad_ref,
    kgrad_ref,
    vgrad_ref,
    kv,
    kv_t,
    queries,
    grads,
    scores,
    dprobs,
    peak,
    probs,
    dscores,
    acc,
    own,
    snd,
    rcv,
    local_sem,
    load_sem,
    fetch_send,
    fetch_recv,
    back_send,
    back_recv,
):
    index = lax.axis_index("ctx")
    run = lax.div(index, RUN)
    place = lax.rem(index, RUN)
    after = lax.rem(run + 1, runs)
    before = lax.rem(run + runs - 1, runs)
    ahead = (1, -1)
    room = (RUN - 1 - place, place)
    trees = ((UP, 0), (DOWN, 1), (UP, 1), (DOWN, 0))
    receivers_run = {(UP, 0): run, (UP, 1): before, (DOWN, 0): after, (DOWN, 1): run}
    owners_run = {(UP, 0): run, (UP, 1): after, (DOWN, 0): before, (DOWN, 1): run}

    def copy(src, dst, send, recv, target):
        return pltpu.make_async_remote_copy(
            src_ref=src,
            dst_ref=dst,
            send_sem=send,
            recv_sem=recv,
            device_id={"ctx": target},
            device_id_type=pl.DeviceIdType.MESH,
        )

    kv_loads = []
    for piece in range(2):
        for part, source in enumerate((k_hbm, v_hbm)):
            kv_loads.append(
                pltpu.make_async_copy(
                    source.at[piece], kv.at[piece, place, part], local_sem.at[piece, part]
                )
            )
    for load in kv_loads:
        load.start()
    loads = []
    for piece in range(2):
        for which, (source, target) in enumerate(((q_hbm, queries), (g_hbm, grads))):
            for head in range(GROUP):
                span = pl.ds(head * TOK, TOK)
                loads.append(
                    pltpu.make_async_copy(
                        source.at[piece, :, span],
                        target.at[piece, span],
                        load_sem.at[piece, which, head],
                    )
                )
    for load in loads:
        load.start()

    barrier = pltpu.get_barrier_semaphore()

    for direction in (UP, DOWN):
        for away in (1, 2):

            @pl.when(room[direction] >= away)
            def _(direction=direction, away=away):
                for at_run in (run, receivers_run[direction, 1 - direction]):
                    pl.semaphore_signal(
                        barrier,
                        inc=1,
                        device_id={"ctx": at_run * RUN + place + ahead[direction] * away},
                        device_id_type=pl.DeviceIdType.MESH,
                    )

    peers = 2 * (jnp.minimum(room[UP], 2) + jnp.minimum(room[DOWN], 2))
    pl.semaphore_wait(barrier, peers)

    for load in kv_loads:
        load.wait()

    def fetch(direction, piece, part, distance, slot, at_run, away):
        return copy(
            kv.at[piece, slot, part],
            kv.at[piece, slot, part],
            fetch_send.at[direction, piece, part, distance],
            fetch_recv.at[direction, piece, part, distance],
            at_run * RUN + place + ahead[direction] * away,
        )

    def send_own(piece):
        for away in (2, 1):
            for part in range(2):
                for direction in (UP, DOWN):

                    @pl.when(room[direction] >= away)
                    def _(direction=direction, part=part, away=away):
                        at_run = receivers_run[direction, piece]
                        fetch(direction, piece, part, away, place, at_run, away).start()

    send_own(0)

    def doc_of(piece, run_of_slot, slot):
        at = run_of_slot * RUN + slot
        inside = (at >= 0) & (at < runs * RUN)
        at = jnp.clip(at, 0, runs * RUN - 1)
        block = at if piece == 0 else 2 * runs * RUN - 1 - at
        return jnp.where(inside, doc_ref[block], -1)

    my_docs = [doc_of(piece, run, place) for piece in range(2)]
    key_row = lax.broadcasted_iota(jnp.int32, (TOK, WIDE), 0)
    query_row = lax.rem(lax.broadcasted_iota(jnp.int32, (TOK, WIDE), 1), TOK)
    causal = key_row <= query_row

    def visit(piece, slot, is_own):
        keys = kv[piece, slot, 0]
        vals = kv[piece, slot, 1]
        kv_t[piece, 0, :, rows_of(slot)] = keys.T
        kv_t[piece, 1, :, rows_of(slot)] = vals.T
        if not is_own:
            if piece == 0:
                run_of_slot = jnp.where(slot > place, run - 1, run)
            else:
                run_of_slot = jnp.where(slot < place, run + 1, run)
            doc = doc_of(piece, run_of_slot, slot)
            bias = jnp.where(doc == my_docs[piece], 0.0, MASKED)
        for first in range(0, COLS, WIDE):
            cols = pl.ds(first, WIDE)
            block = dot(keys, queries[piece, cols], 1, 1)
            if is_own:
                block = jnp.where(causal, block, MASKED)
            else:
                block = block + bias
            scores[piece, rows_of(slot), cols] = block
            top = jnp.max(block.reshape(TOK // 8, 8, WIDE), axis=0)
            if not is_own:
                top = jnp.maximum(top, peak[piece, :, cols])
            peak[piece, :, cols] = top
            dprobs[piece, rows_of(slot), cols] = dot(vals, grads[piece, cols], 1, 1)

    for load in loads:
        load.wait()
    for piece in range(2):
        visit(piece, place, True)

    def slot_at(direction, distance):
        return place - ahead[direction] * distance, room[1 - direction] >= distance

    def fetch_step(piece, step):
        for even in (1, 0):
            distance = 2 * step + 1 + even
            for part in range(2):
                for direction in (UP, DOWN):
                    slot, present = slot_at(direction, distance)

                    @pl.when(present)
                    def _(direction=direction, part=part, slot=slot, distance=distance, even=even):
                        fetch(direction, piece, part, distance, slot, run, 1).wait_recv()
                        if not even:
                            return
                        for away in (2, 1):

                            @pl.when(room[direction] >= away)
                            def _(away=away):
                                fetch(
                                    direction, piece, part, distance + away, slot, run, away
                                ).start()

        def visit_pair(which, carry):
            for direction in (UP, DOWN):
                slot, present = slot_at(direction, 2 * step + 1 + which)

                @pl.when(present)
                def _(slot=slot):
                    visit(piece, slot, False)

            return carry

        lax.fori_loop(0, 2, visit_pair, 0)

    def soften(piece, group):
        cols = pl.ds(pl.multiple_of(group * WIDE, WIDE), WIDE)
        top = jnp.max(peak[piece, :, cols], axis=0, keepdims=True)
        total = jnp.zeros((8, WIDE), jnp.float32)
        delta = jnp.zeros((8, WIDE), jnp.float32)
        for slot in range(RUN):
            rows = pl.ds(slot * TOK, TOK)
            weight = jnp.exp2((scores[piece, rows, cols] - top) * EXP2_SCALE)
            scores[piece, rows, cols] = weight
            total += jnp.sum(weight.reshape(TOK // 8, 8, WIDE), axis=0)
            delta += jnp.sum(
                (weight * dprobs[piece, rows, cols]).reshape(TOK // 8, 8, WIDE), axis=0
            )
        inverse = 1.0 / jnp.sum(total, axis=0, keepdims=True)
        delta = jnp.sum(delta, axis=0, keepdims=True) * inverse
        for slot in range(RUN):
            rows = pl.ds(slot * TOK, TOK)
            prob = scores[piece, rows, cols] * inverse
            probs[piece, rows, cols] = prob.astype(jnp.bfloat16)
            dscores[piece, rows, cols] = (prob * (dprobs[piece, rows, cols] - delta)).astype(
                jnp.bfloat16
            )

    def key_side(piece, slot):
        rows = rows_of(slot)
        return (
            dot(dscores[piece, rows, :], queries[piece], 1, 0) * SCALE,
            dot(probs[piece, rows, :], grads[piece], 1, 0),
        )

    def back(direction, piece, part, distance, slot, even, owner_is_next):
        at_run = jnp.where(owner_is_next, owners_run[direction, piece], run)
        return copy(
            snd.at[piece, slot, part],
            rcv.at[direction, piece, even, slot, part],
            back_send.at[direction, piece, part, distance],
            back_recv.at[direction, piece, part, distance],
            at_run * RUN + place - ahead[direction] * (1 + even),
        )

    def odd_step(piece, step):
        distance = RUN - 1 - 2 * step
        for direction in (UP, DOWN):
            slot, present = slot_at(direction, distance)

            @pl.when(present)
            def _(direction=direction, slot=slot):
                for part, value in enumerate(key_side(piece, slot)):
                    snd[piece, slot, part] = value.astype(jnp.bfloat16)
                    back(direction, piece, part, distance, slot, 0, distance == 1).start()

    def gather(total, direction, piece, part, distance, slot):
        for even in (0, 1):

            @pl.when(room[direction] > even)
            def _(even=even):
                child = distance + 1 + even
                back(direction, piece, part, child, slot, even, False).wait_recv()
                total[...] += rcv[direction, piece, even, slot, part].astype(jnp.float32)

    def even_step(piece, step):
        distance = RUN - 2 - 2 * step
        for direction in (UP, DOWN):
            slot, present = slot_at(direction, distance)

            @pl.when(present)
            def _(direction=direction, slot=slot):
                for part, value in enumerate(key_side(piece, slot)):
                    acc[direction, piece, part] = value

        for part in range(2):
            for direction in (UP, DOWN):
                slot, present = slot_at(direction, distance)

                @pl.when(present)
                def _(direction=direction, part=part, slot=slot):
                    total = acc.at[direction, piece, part]
                    gather(total, direction, piece, part, distance, slot)
                    snd[piece, slot, part] = total[...].astype(jnp.bfloat16)
                    back(direction, piece, part, distance, slot, 1, distance == 2).start()

    def query_side(piece, group):
        cols = pl.ds(pl.multiple_of(group * WIDE, WIDE), WIDE)
        attended = dot(kv_t[piece, 1], probs[piece, :, cols], 1, 0)
        out_ref[piece, :, cols] = jnp.concatenate(
            [attended[:, :TOK].T, attended[:, TOK:].T], axis=1
        ).astype(jnp.bfloat16)
        pulled = dot(kv_t[piece, 0], dscores[piece, :, cols], 1, 0) * SCALE
        qgrad_ref[piece, :, cols] = jnp.concatenate(
            [pulled[:, :TOK].T, pulled[:, TOK:].T], axis=1
        ).astype(jnp.bfloat16)

    def finish(piece):
        for part, value in enumerate(key_side(piece, place)):
            own[piece, part] = value
        repeat(COLS // WIDE, query_side, piece)
        for part in range(2):
            for direction in (UP, DOWN):
                gather(own.at[piece, part], direction, piece, part, 0, place)
        kgrad_ref[piece] = own[piece, 0].astype(jnp.bfloat16)
        vgrad_ref[piece] = own[piece, 1].astype(jnp.bfloat16)

    def repeat(count, action, piece):
        def body(step, carry):
            action(piece, step)
            return carry

        lax.fori_loop(0, count, body, 0)

    def stage(time, carry):
        @pl.when(time == LAG - 1)
        def _():
            send_own(1)

        for piece in range(2):
            now = time - LAG * piece
            @pl.when((now >= 0) & (now < RUN // 2))
            def _(piece=piece, now=now):
                fetch_step(piece, now)

            @pl.when(now == RUN // 2 - 1)
            def _(piece=piece):
                repeat(COLS // WIDE, soften, piece)
                repeat(RUN // 2, odd_step, piece)

            @pl.when((now >= RUN // 2) & (now < RUN - 1))
            def _(piece=piece, now=now):
                even_step(piece, now - RUN // 2)

            @pl.when(now == RUN - 1)
            def _(piece=piece):
                finish(piece)

        return carry

    lax.fori_loop(0, RUN + LAG, stage, 0)

    def drain(step, carry):
        distance = step + 1
        away = 1 + lax.rem(step, 2)
        for direction, piece in trees:
            for part in range(2):

                @pl.when((room[1 - direction] >= distance - away) & (room[direction] >= away))
                def _(direction=direction, piece=piece, part=part):
                    fetch(direction, piece, part, distance, place, run, 1).wait_send()

                @pl.when(room[1 - direction] >= distance)
                def _(direction=direction, piece=piece, part=part):
                    back(direction, piece, part, distance, place, 0, False).wait_send()

        return carry

    lax.fori_loop(0, RUN - 1, drain, 0)


def local(queries, keys, values, out_grad, block_doc):
    runs = lax.axis_size("ctx") // RUN
    bf16, f32 = jnp.bfloat16, jnp.float32
    wide = (2, TOK, COLS)
    thin = (2, TOK, HD)
    any_space = pl.BlockSpec(memory_space=pltpu.HBM)
    vmem = pl.BlockSpec(memory_space=pltpu.VMEM)
    dma = pltpu.SemaphoreType.DMA
    results = pl.pallas_call(
        functools.partial(kernel, runs),
        out_shape=[
            jax.ShapeDtypeStruct(wide, bf16),
            jax.ShapeDtypeStruct(wide, bf16),
            jax.ShapeDtypeStruct(thin, bf16),
            jax.ShapeDtypeStruct(thin, bf16),
        ],
        in_specs=[pl.BlockSpec(memory_space=pltpu.SMEM)] + [any_space] * 4,
        out_specs=[vmem] * 4,
        scratch_shapes=[
            pltpu.VMEM((2, RUN, 2, TOK, HD), bf16),
            pltpu.VMEM((2, 2, HD, RUN * TOK), bf16),
            pltpu.VMEM((2, COLS, HD), bf16),
            pltpu.VMEM((2, COLS, HD), bf16),
            pltpu.VMEM((2, RUN * TOK, COLS), f32),
            pltpu.VMEM((2, RUN * TOK, COLS), f32),
            pltpu.VMEM((2, 8, COLS), f32),
            pltpu.VMEM((2, RUN * TOK, COLS), bf16),
            pltpu.VMEM((2, RUN * TOK, COLS), bf16),
            pltpu.VMEM((2, 2, 2, TOK, HD), f32),
            pltpu.VMEM((2, 2, TOK, HD), f32),
            pltpu.VMEM((2, RUN, 2, TOK, HD), bf16),
            pltpu.VMEM((2, 2, 2, RUN, 2, TOK, HD), bf16),
            dma((2, 2)),
            dma((2, 2, GROUP)),
            dma((2, 2, 2, RUN)),
            dma((2, 2, 2, RUN)),
            dma((2, 2, 2, RUN)),
            dma((2, 2, 2, RUN)),
        ],
        compiler_params=pltpu.CompilerParams(
            collective_id=0, has_side_effects=True, vmem_limit_bytes=VMEM_LIMIT
        ),
    )(
        block_doc,
        queries.reshape(wide),
        keys.reshape(thin),
        values.reshape(thin),
        out_grad.reshape(wide),
    )
    return tuple(array[:, None] for array in results)


def solution(mesh):
    spec = P(None, "ctx", None, "tp")
    return jax.shard_map(
        local,
        mesh=mesh,
        in_specs=(spec, spec, spec, spec, P()),
        out_specs=(spec, spec, spec, spec),
        check_vma=False,
    )
```
